32 devices in a mesh: parts: 2 (over y), row: 4 (over x, core), col: 4 (over z).
Axes of the slice: x: 2, y: 2, z: 4, core: 2. Of those that a mesh axis runs over, the one named last changes fastest.
Arguments:
- latent: bfloat16 [4, 32, 32, 640], P('parts', 'row', 'col'), parts along dimension 0, may hold values from -6 to 6
- timestep: int32 [4], P('parts'), parts along dimension 0, may hold values from 0 to 999
- gn_gain: float32 [640], replicated, may hold values from 0.25 to 1.75
- gn_bias: float32 [640], replicated, may hold values from -3 to 3
- conv_weight: bfloat16 [3, 3, 640, 640], P(None, None, None, 'row'), may hold values from -0.078125 to 0.078125
- conv_bias: float32 [640], replicated, may hold values from -3 to 3
- time_weight: bfloat16 [320, 640], replicated, may hold values from -0.625 to 0.625
- ln_gain: float32 [640], replicated, may hold values from 0.25 to 1.75
- q_weight: bfloat16 [640, 384], replicated, may hold values from -0.5 to 0.5
- k_weight: bfloat16 [640, 384], replicated, may hold values from -0.25 to 0.25
- v_weight: bfloat16 [640, 384], replicated, may hold values from -0.25 to 0.25
- out_weight: bfloat16 [384, 640], replicated, may hold values from -0.3125 to 0.3125
- stale_keys: bfloat16 [4, 32, 32, 384], P('parts', 'row', 'col'), parts along dimension 0, may hold values from -40 to 40
- stale_values: bfloat16 [4, 32, 32, 384], P('parts', 'row', 'col'), parts along dimension 0, may hold values from -6 to 6
Outputs:
- mixed: bfloat16 [4, 32, 32, 640], P('parts', 'row', 'col'), parts along dimension 0
- fresh_keys: bfloat16 [4, 32, 32, 384], P('parts', 'row', 'col'), parts along dimension 0
- fresh_values: bfloat16 [4, 32, 32, 384], P('parts', 'row', 'col'), parts along dimension 0
The draws below stay inside these ranges and needn't reach their ends.
There are 2 independent parts, one for each index of `parts`. The reference program is written for one: setup_inputs(seed, part) draws one part's arguments, and reference() takes and returns one part's arrays. A program takes and returns all parts, laid end to end along the dimension named above; an argument that names none is the same for every part. Nothing has to cross between parts.
All inputs are finite; a program needn't handle non-finite values.
Results may differ from the reference program's by a relative error of at most 0.012.
Values may be sent and summed in bfloat16 or wider, within the bound.
A program may use at most 64 MiB of HBM per device.

```python
import jax
import jax.numpy as jnp
from jax import lax

C = 640
NH = 6
HD = 64
GROUPS = 32
TDIM = 320
IMAGE_GROUP_SIZE = 2
RD = 8
CD = 8
GRID_HEIGHT = 32
GRID_WIDTH = 32
INNER = 384
N_ROW = 4
N_COL = 4


def draw_stale_keys(key, part):
    first = jax.random.fold_in(key, 0)
    shape = (IMAGE_GROUP_SIZE, GRID_HEIGHT, GRID_WIDTH, NH * HD)
    result = jnp.clip(jax.random.normal(first, shape, jnp.float32), -6.0, 6.0)
    return result.astype(jnp.bfloat16)


def draw_q_weight(key, part):
    first = jax.random.fold_in(key, 0)
    scale = 1.0 / jnp.sqrt(jnp.float32(C))
    starting_level = jnp.clip(jax.random.normal(first, (C, NH * HD), jnp.float32), -6.0, 6.0) * scale
    return jnp.clip(starting_level, -0.5, 0.5).astype(jnp.bfloat16)


def block_levels(stream_key, shape, pieces, least, high):
    level = 1.0
    for dim, parts in pieces:
        heights = jax.random.uniform(jax.random.fold_in(jax.random.fold_in(stream_key, 6), dim), (parts,), jnp.float32, least / len(pieces), high / len(pieces))
        level = level * jnp.repeat(jnp.exp(heights), shape[dim] // parts).reshape((-1,) + (1,) * (len(shape) - 1 - dim))
    return level


def scatter_about(stream_key, extent, scale, limit, cuts=(), held_as=jnp.bfloat16):
    values = scale * jax.random.normal(stream_key, extent, jnp.float32)
    if cuts:
        values = values * block_levels(stream_key, extent, cuts, -0.22, 0.18)
    return jnp.clip(values, -limit, limit).astype(held_as)


def setup_inputs(seed: int = 0, part: int = 0) -> dict:
    keys = jax.random.split(jax.random.key(seed), 15)
    part_splits = jax.random.split(jax.random.fold_in(keys[14], part), 15)
    latent = scatter_about(part_splits[0], (IMAGE_GROUP_SIZE, GRID_HEIGHT, GRID_WIDTH, C), 1.0, 6.0, ((1, 4), (2, 4)))
    timestep = jax.random.randint(part_splits[1], (IMAGE_GROUP_SIZE,), 0, 1000).astype(jnp.int32)
    gn_gain = jnp.clip(1.0 + 0.15 * jax.random.normal(keys[2], (C,), jnp.float32), 0.25, 1.75)
    gn_bias = scatter_about(keys[3], (C,), 0.5, 3.0, (), jnp.float32)
    conv_weight = scatter_about(keys[4], (3, 3, C, C), (9 * C) ** -0.5, 0.078125, ((3, 4),))
    conv_bias = scatter_about(keys[5], (C,), 0.5, 3.0, (), jnp.float32)
    time_weight = scatter_about(keys[6], (TDIM, C), (TDIM // 4) ** -0.5, 0.625)
    ln_gain = jnp.clip(1.0 + 0.15 * jax.random.normal(keys[7], (C,), jnp.float32), 0.25, 1.75)
    q_weight = draw_q_weight(jax.random.fold_in(keys[14], 71), part)
    k_weight = scatter_about(keys[9], (C, INNER), C ** -0.5, 0.25)
    v_weight = scatter_about(keys[10], (C, INNER), C ** -0.5, 0.25)
    out_weight = scatter_about(keys[11], (INNER, C), INNER ** -0.5, 0.3125)
    stale_keys = draw_stale_keys(jax.random.fold_in(jax.random.fold_in(keys[14], part), 71), part)
    stale_values = scatter_about(part_splits[13], (IMAGE_GROUP_SIZE, GRID_HEIGHT, GRID_WIDTH, INNER), 1.0, 6.0, ((1, 4), (2, 4)))
    return dict(latent=latent, timestep=timestep, gn_gain=gn_gain, gn_bias=gn_bias, conv_weight=conv_weight, conv_bias=conv_bias, time_weight=time_weight, ln_gain=ln_gain, q_weight=q_weight, k_weight=k_weight, v_weight=v_weight, out_weight=out_weight, stale_keys=stale_keys, stale_values=stale_values)


def time_features(timestep):
    half = TDIM // 2
    freqs = jnp.exp(-jnp.log(10000.0) * jnp.arange(half, dtype=jnp.float32) / half)
    angles = timestep.astype(jnp.float32)[:, None] * freqs[None, :]
    return jnp.concatenate([jnp.cos(angles), jnp.sin(angles)], axis=1)

def to_patches(array):
    batch = array.shape[0]
    shaped = array.reshape(batch, N_ROW, RD, N_COL, CD, NH, HD)
    return shaped.transpose(0, 1, 3, 2, 4, 5, 6).reshape(batch, N_ROW * N_COL, RD * CD, NH, HD)

def from_patches(array):
    batch = array.shape[0]
    shaped = array.reshape(batch, N_ROW, N_COL, RD, CD, NH * HD)
    return shaped.transpose(0, 1, 3, 2, 4, 5).reshape(batch, GRID_HEIGHT, GRID_WIDTH, NH * HD)

def one_image(items):
    query_p, fresh_kp, fresh_vp, stale_k, stale_v = items
    patches = query_p.shape[0]
    span = query_p.shape[1]
    keys_flat = stale_k.reshape(patches * span, NH, HD).astype(jnp.float32)
    values_flat = stale_v.reshape(patches * span, NH, HD).astype(jnp.float32)
    owner = jnp.arange(patches * span, dtype=jnp.int32) // span

    def one_patch(index):
        query = query_p[index].astype(jnp.float32)
        fresh_k = fresh_kp[index].astype(jnp.float32)
        fresh_v = fresh_vp[index].astype(jnp.float32)
        masked = (owner == index)[None, None, :]
        scores = jnp.einsum('qhd,khd->hqk', query, keys_flat)
        scores = jnp.where(masked, -1e+30, scores)
        own_scores = jnp.einsum('qhd,khd->hqk', query, fresh_k)
        peak = jnp.maximum(lax.optimization_barrier(jnp.max(scores, axis=-1)), lax.optimization_barrier(jnp.max(own_scores, axis=-1)))
        weights = jnp.where(masked, 0.0, jnp.exp(scores - peak[..., None]))
        own_weights = jnp.exp(own_scores - peak[..., None])
        total = lax.optimization_barrier(jnp.sum(weights, axis=-1)) + lax.optimization_barrier(jnp.sum(own_weights, axis=-1))
        rounded = weights.astype(jnp.bfloat16).astype(jnp.float32)
        own_rounded = own_weights.astype(jnp.bfloat16).astype(jnp.float32)
        summed = jnp.einsum('hqk,khd->hqd', rounded, values_flat) + jnp.einsum('hqk,khd->hqd', own_rounded, fresh_v)
        result = summed / total[..., None]
        return result.transpose(1, 0, 2).reshape(span, NH * HD).astype(jnp.bfloat16)
    return lax.map(one_patch, jnp.arange(patches, dtype=jnp.int32))

def reference(latent, timestep, gn_gain, gn_bias, conv_weight, conv_bias, time_weight, ln_gain, q_weight, k_weight, v_weight, out_weight, stale_keys, stale_values):
    batch = latent.shape[0]
    emb = jax.nn.silu(time_features(timestep)).astype(jnp.bfloat16)
    temb = jnp.dot(emb, time_weight, preferred_element_type=jnp.float32)
    values = latent.astype(jnp.float32)
    grouped = values.reshape(batch, GRID_HEIGHT * GRID_WIDTH, GROUPS, C // GROUPS)
    mean = lax.optimization_barrier(jnp.mean(grouped, axis=(1, 3)))
    var = lax.optimization_barrier(jnp.mean(grouped * grouped, axis=(1, 3))) - mean * mean
    normed = (grouped - mean[:, None, :, None]) * lax.rsqrt(var + 1e-05)[:, None, :, None]
    normed = normed.reshape(batch, GRID_HEIGHT, GRID_WIDTH, C) * gn_gain + gn_bias
    act = jax.nn.silu(normed).astype(jnp.bfloat16)
    padded = jnp.pad(act, ((0, 0), (1, 1), (1, 1), (0, 0)))
    conv = jnp.zeros((batch, GRID_HEIGHT, GRID_WIDTH, C), jnp.float32)
    for down in range(3):
        for across in range(3):
            conv = conv + jnp.dot(padded[:, down:down + GRID_HEIGHT, across:across + GRID_WIDTH, :], conv_weight[down, across], preferred_element_type=jnp.float32)
    hidden = (values + conv + conv_bias + temb[:, None, None, :]).astype(jnp.bfloat16)
    hidden_f = hidden.astype(jnp.float32)
    centre = hidden_f - lax.optimization_barrier(jnp.mean(hidden_f, axis=-1, keepdims=True))
    spread = lax.optimization_barrier(jnp.mean(centre * centre, axis=-1, keepdims=True))
    layer_normed = (centre * lax.rsqrt(spread + 1e-05) * ln_gain).astype(jnp.bfloat16)
    queries = (jnp.dot(layer_normed, q_weight, preferred_element_type=jnp.float32) * (1.0 / jnp.sqrt(jnp.float32(HD)))).astype(jnp.bfloat16)
    fresh_keys = jnp.dot(layer_normed, k_weight, preferred_element_type=jnp.float32).astype(jnp.bfloat16)
    fresh_values = jnp.dot(layer_normed, v_weight, preferred_element_type=jnp.float32).astype(jnp.bfloat16)
    attended = lax.map(one_image, (to_patches(queries), to_patches(fresh_keys), to_patches(fresh_values), to_patches(stale_keys), to_patches(stale_values)))
    attn = from_patches(attended)
    mixed = (hidden_f + jnp.dot(attn, out_weight, preferred_element_type=jnp.float32)).astype(jnp.bfloat16)
    return (mixed, fresh_keys, fresh_values)
```

```python
import functools

import jax
import jax.numpy as jnp
from jax import lax
from jax.experimental import pallas as pl
from jax.experimental.pallas import tpu as pltpu
from jax.sharding import PartitionSpec as P

HD = 64
GROUPS = 32
PAIR = 2
MESH = pl.DeviceIdType.MESH
F32 = jnp.float32
BF16 = jnp.bfloat16


def group_total(sums, size):
    width = sums.shape[1]
    lane = lax.broadcasted_iota(jnp.int32, sums.shape, 1)

    def window(x, sign):
        parts, total, offset = {1: x}, None, 0
        step = 1
        while step * 2 <= size:
            last = parts[step]
            parts[step * 2] = last + pltpu.roll(last, (sign * step) % width, 1)
            step *= 2
        for step in sorted(parts, reverse=True):
            if size & step:
                piece = parts[step]
                if offset:
                    piece = pltpu.roll(piece, (sign * offset) % width, 1)
                total = piece if total is None else total + piece
                offset += step
        return total

    ends = jnp.where(lax.rem(lane, size) == size - 1, window(sums, 1), 0.0)
    return window(ends, -1)


def finish(a, b, c, x, y, z, sem):
    copies = [pltpu.make_async_copy(p, q, sem.at[n]) for n, (p, q) in enumerate(((a, x), (b, y), (c, z)))]
    for copy in copies:
        copy.start()
    for copy in copies:
        copy.wait()


def silu(y):
    half = 0.5 * y
    return half + half * jnp.tanh(half)


def kernel(
    dims,
    t_hbm,
    gg_hbm,
    gb_hbm,
    lg_hbm,
    bias_hbm,
    lat_hbm,
    tw_hbm,
    cw_hbm,
    qw_hbm,
    kw_hbm,
    vw_hbm,
    ow_hbm,
    sk_hbm,
    sv_hbm,
    mixed_ref,
    fk_ref,
    fv_ref,
    t_ref,
    gg_ref,
    gb_ref,
    lg_ref,
    bias_ref,
    band,
    edges,
    halo,
    tw,
    acts,
    cw,
    qkvw,
    ow,
    rstats,
    cstats,
    hsend,
    hbuf,
    hfull,
    kbuf,
    vbuf,
    qown,
    qin,
    own_o,
    own_s,
    out_o,
    in_o,
    attn,
    load_sem,
    row_send,
    row_recv,
    col_send,
    col_recv,
    hop_send,
    hop_recv,
    edge_send,
    edge_recv,
    fwd_send,
    fwd_recv,
    x_send,
    x_recv,
):
    R, C, NX, rows, cols, channels, inner, count_all = dims
    span = rows * cols
    wide = channels // R
    nb = 2
    me = lax.axis_index("row")
    mc = lax.axis_index("col")

    def remote(src, dst, send, recv, **where):
        return pltpu.make_async_remote_copy(
            src_ref=src, dst_ref=dst, send_sem=send, recv_sem=recv, device_id=where, device_id_type=MESH
        )

    def local(n, src, dst):
        return pltpu.make_async_copy(src, dst, load_sem.at[n])

    own_load = local(0, lat_hbm, band.at[me])
    own_load.start()
    barrier = pltpu.get_barrier_semaphore()
    for d in range(1, C):
        pl.semaphore_signal(barrier, inc=1, device_id={"col": lax.rem(mc + d, C)}, device_id_type=MESH)
    for d in range(1, R):
        pl.semaphore_signal(barrier, inc=1, device_id={"row": lax.rem(me + d, R)}, device_id_type=MESH)
    load_k = local(1, sk_hbm, kbuf.at[:, 0:span])
    load_v = local(2, sv_hbm, vbuf.at[:, 0:span])
    load_t = [local(3, t_hbm, t_ref), local(4, bias_hbm, bias_ref), local(5, tw_hbm, tw)]
    load_gn = [local(6, gg_hbm, gg_ref), local(7, gb_hbm, gb_ref)]
    load_cw = local(8, cw_hbm, cw)
    load_q = [local(9, lg_hbm, lg_ref), local(10, qw_hbm, qkvw.at[:, 0:inner])]
    load_kv = [
        local(11, kw_hbm, qkvw.at[:, inner : 2 * inner]),
        local(12, vw_hbm, qkvw.at[:, 2 * inner : 3 * inner]),
    ]
    load_ow = local(13, ow_hbm, ow)
    for copy in [load_k, load_v] + load_t + load_gn + [load_cw] + load_q + load_kv + [load_ow]:
        copy.start()

    mate = me + 1 - 2 * lax.rem(me, PAIR)
    started = []

    def go(src, dst, send, recv, **where):
        copy = remote(src, dst, send, recv, **where)
        copy.start()
        started.append(copy)
        return copy

    own_load.wait()
    sums = [[], []]
    for b in range(nb):
        x = band[me, b].astype(F32)
        edges[0, b] = x[:, cols - 1, :].astype(BF16)
        edges[1, b] = x[:, 0, :].astype(BF16)
        flat = x.reshape(span, channels)
        sums[0].append(jnp.sum(flat, axis=0, keepdims=True))
        sums[1].append(jnp.sum(flat * flat, axis=0, keepdims=True))
    sums = jnp.concatenate(sums[0] + sums[1] + sums[0] + sums[1], axis=0)
    rstats[0] = group_total(sums, channels // GROUPS) * (1.0 / count_all)

    pl.semaphore_wait(barrier, R - 1 + C - 1)

    to_right = remote(edges.at[0], halo.at[me, 0], edge_send.at[0], edge_recv.at[0], col=lax.rem(mc + 1, C))
    to_left = remote(edges.at[1], halo.at[me, 1], edge_send.at[1], edge_recv.at[1], col=lax.rem(mc + C - 1, C))

    @pl.when(mc < C - 1)
    def _():
        to_right.start()

    @pl.when(mc > 0)
    def _():
        to_left.start()

    row_stats = [
        go(rstats.at[0], rstats.at[R - d], row_send.at[nb + 2, d], row_recv.at[nb + 2, d], row=lax.rem(me + d, R))
        for d in range(1, R)
    ]

    def spread(ref, n):
        cross = [
            go(ref, ref, row_send.at[n, k], row_recv.at[n, k], row=lax.rem(me + k * PAIR, R)) for k in range(1, NX)
        ]
        return [go(ref, ref, row_send.at[n, 0], row_recv.at[n, 0], row=mate)], cross

    def relay(cross, at, n):
        handed = []
        for k in range(1, NX):
            cross[k - 1].wait_recv()
            ref = at(lax.rem(me + R - k * PAIR, R))
            handed.append(go(ref, ref, row_send.at[n, NX - 1 + k], row_recv.at[n, NX - 1 + k], row=mate))
        return handed

    lat_out = [spread(band.at[me, b], b) for b in range(nb)]

    def hops(k, b):
        made = []
        for way, slot, dest, to, sends, takes in (
            (0, (C - k + 1) % C, C - k, mc + 1, (mc >= k - 1) & (mc < C - 1), mc >= k),
            (1, k - 1, k, mc + C - 1, (mc <= C - k) & (mc > 0), mc <= C - 1 - k),
        ):
            pair = [
                remote(
                    buf.at[b, slot * span : (slot + 1) * span],
                    buf.at[b, dest * span : (dest + 1) * span],
                    hop_send.at[k, n, way, b],
                    hop_recv.at[k, n, way, b],
                    col=lax.rem(to, C),
                )
                for n, buf in enumerate((kbuf, vbuf))
            ]
            made.append((pair, sends, takes))
        return made

    def each(k, b, act, which):
        for hop in hops(k, b):

            @pl.when(hop[which])
            def _(pair=hop[0]):
                for copy in pair:
                    act(copy)

    def send_hop(k, b):
        if k > 1:
            each(k - 1, b, lambda copy: copy.wait_recv(), 2)
        each(k, b, lambda copy: copy.start(), 1)

    waiting = [(k, b) for k in range(2, C) for b in range(nb)]

    def advance(n):
        for _ in range(min(n, len(waiting))):
            send_hop(*waiting.pop(0))

    load_k.wait()
    load_v.wait()
    for b in range(nb):
        send_hop(1, b)

    half_t = tw.shape[0] // 2
    for copy in load_t:
        copy.wait()
    line = lax.broadcasted_iota(jnp.int32, (nb * cols, half_t), 0)
    when = jnp.where(line < cols, t_ref[0], t_ref[1]).astype(F32)
    place_t = lax.broadcasted_iota(jnp.int32, (nb * cols, half_t), 1).astype(F32)
    angles = when * jnp.exp(-jnp.log(jnp.full((1, 1), 10000.0, F32)) * place_t / half_t)
    temb = jnp.dot(
        jax.nn.silu(jnp.cos(angles)).astype(BF16), tw[0:half_t, :], preferred_element_type=F32
    ) + jnp.dot(jax.nn.silu(jnp.sin(angles)).astype(BF16), tw[half_t:, :], preferred_element_type=F32)
    temb = temb + bias_ref[...].reshape(1, channels)
    own = jnp.concatenate([band[me, b].astype(F32) for b in range(nb)], axis=1)
    hfull[...] = (own + temb[None]).reshape(nb * span, channels)

    for copy in row_stats:
        copy.wait_recv()
    cstats[0] = functools.reduce(lambda p, q: p + q, [rstats[d] for d in range(R)])
    col_stats = [
        go(cstats.at[0], cstats.at[C - d], col_send.at[0, d], col_recv.at[0, d], col=lax.rem(mc + d, C))
        for d in range(1, C)
    ]

    @pl.when(mc == 0)
    def _():
        halo[me, 0] = jnp.zeros(halo.shape[2:], BF16)

    @pl.when(mc == C - 1)
    def _():
        halo[me, 1] = jnp.zeros(halo.shape[2:], BF16)

    @pl.when(mc > 0)
    def _():
        to_right.wait_recv()

    @pl.when(mc < C - 1)
    def _():
        to_left.wait_recv()

    halo_out = spread(halo.at[me], nb)
    for t in range(3):
        acts[t, 0] = jnp.zeros(acts.shape[2:], BF16)
        acts[t, R * rows + 1] = jnp.zeros(acts.shape[2:], BF16)
    handed = []
    for b in range(nb):
        handed += relay(lat_out[b][1], lambda p, b=b: band.at[p, b], b)
    handed += relay(halo_out[1], lambda p: halo.at[p], nb)
    advance(nb)
    for copy in load_gn:
        copy.wait()
    for b in range(nb):
        lat_out[b][0][0].wait_recv()
    halo_out[0][0].wait_recv()
    for copy in col_stats:
        copy.wait_recv()
    total = functools.reduce(lambda p, q: p + q, [cstats[d] for d in range(C)])
    mean = [total[b : b + 1] for b in range(nb)]
    gain = gg_ref[...].reshape(1, channels)
    scale = [lax.rsqrt(total[nb + b : nb + b + 1] - mean[b] * mean[b] + 1e-05) * gain for b in range(nb)]
    shift = [gb_ref[...].reshape(1, channels) - mean[b] * scale[b] for b in range(nb)]
    for copy in handed:
        copy.wait_recv()

    def activate(x, b):
        return silu(x.astype(F32) * scale[b] + shift[b])

    place = lax.broadcasted_iota(jnp.int32, (rows, cols, channels), 1)
    for r in range(R):
        tap = [[], [], []]
        for b in range(nb):
            a = activate(band[r, b], b)
            left = jnp.where(mc > 0, activate(halo[r, 0, b], b), 0.0)
            right = jnp.where(mc < C - 1, activate(halo[r, 1, b], b), 0.0)
            tap[0].append(jnp.where(place == 0, left[:, None, :], pltpu.roll(a, 1, 1)))
            tap[1].append(a)
            tap[2].append(jnp.where(place == cols - 1, right[:, None, :], pltpu.roll(a, cols - 1, 1)))
        for t in range(3):
            acts[t, 1 + r * rows : 1 + (r + 1) * rows] = jnp.concatenate(tap[t], axis=1).astype(BF16)
    load_cw.wait()
    h_out = []
    for k in list(range(1, NX)) + [0]:
        chip = lax.rem(me // PAIR + k, NX)
        top = chip * (PAIR * rows)
        acc = None
        for across in range(3):
            for down in range(3):
                part = lax.dot_general(
                    acts[across, pl.ds(top + down, PAIR * rows)].reshape(PAIR * rows * nb * cols, channels),
                    cw[down, across],
                    (((1,), (1,)), ((), ())),
                    preferred_element_type=F32,
                )
                acc = part if acc is None else acc + part
        hsend[pl.ds(chip * PAIR, PAIR)] = acc.reshape(PAIR, nb * span, wide).astype(BF16)
        if k:
            for core in range(PAIR):
                to = chip * PAIR + lax.rem(me + core, PAIR)
                n = k * PAIR + core
                h_out.append(go(hsend.at[to], hbuf.at[me], row_send.at[nb + 1, n], row_recv.at[nb + 1, n], row=to))
            advance(1)
    h_out.append(go(hsend.at[mate], hbuf.at[me], row_send.at[nb + 1, 1], row_recv.at[nb + 1, 1], row=mate))
    hbuf[me] = hsend[me]
    advance(len(waiting))
    for copy in load_q:
        copy.wait()
    for copy in h_out:
        copy.wait_recv()
    h = hfull[...] + jnp.concatenate([hbuf[r].astype(F32) for r in range(R)], axis=1)
    h = h.astype(BF16).astype(F32)
    hfull[...] = h
    centre = h - jnp.mean(h, axis=1, keepdims=True)
    spread_h = jnp.mean(centre * centre, axis=1, keepdims=True)
    normed = (centre * lax.rsqrt(spread_h + 1e-05) * lg_ref[...].reshape(1, channels)).astype(BF16)

    def project(first, last):
        out = jnp.dot(normed, qkvw[:, first * inner : last * inner], preferred_element_type=F32)
        return out.reshape(rows, nb, cols, (last - first) * inner)

    queries = project(0, 1)
    q_out = []
    for b in range(nb):
        qown[b] = (queries[:, b].reshape(span, inner) * (1.0 / HD**0.5)).astype(BF16)
        q_out.append(
            [
                go(qown.at[b], qin.at[NX - d, b], x_send.at[b, d], x_recv.at[b, d], row=lax.rem(me + d * PAIR, R))
                for d in range(1, NX)
            ]
        )
    forwards = []

    def forward(b):
        if C > 1:
            each(C - 1, b, lambda copy: copy.wait_recv(), 2)
        forwards.append(
            [
                go(buf.at[b, 0 : C * span], buf.at[b, C * span : 2 * C * span], fwd_send.at[n, b], fwd_recv.at[n, b], row=mate)
                for n, buf in enumerate((kbuf, vbuf))
            ]
        )

    forward(0)
    for copy in load_kv:
        copy.wait()
    fresh = project(1, 3)
    for b in range(nb):
        part = fresh[:, b].reshape(span, 2 * inner)
        k = part[:, :inner].astype(BF16)
        v = part[:, inner:].astype(BF16)
        kbuf[b, 2 * C * span :] = k
        vbuf[b, 2 * C * span :] = v
        fk_ref[b] = k
        fv_ref[b] = v
    for b in range(1, nb):
        forward(b)

    half = lax.broadcasted_iota(jnp.int32, (span, 2 * HD), 1) < HD
    lanes = lax.broadcasted_iota(jnp.int32, (span, 128), 1)
    zero = jnp.zeros((span, 2 * HD), BF16)

    def attend(q, b, start, o_store):
        held = jnp.zeros((span, 128), F32)
        for pair in range(inner // (2 * HD)):
            at = slice(pair * 2 * HD, (pair + 1) * 2 * HD)
            q2 = q[:, at]
            q2 = jnp.concatenate([jnp.where(half, q2, zero), jnp.where(half, zero, q2)], axis=0)
            s = lax.dot_general(
                q2, kbuf[b, start : start + 2 * C * span, at], (((1,), (1,)), ((), ())), preferred_element_type=F32
            )
            m = jnp.max(s, axis=1, keepdims=True).astype(BF16).astype(F32)
            p = jnp.exp(s - m)
            l = jnp.sum(p, axis=1, keepdims=True)
            o = jnp.dot(p.astype(BF16), vbuf[b, start : start + 2 * C * span, at], preferred_element_type=F32)
            o_store(at, jnp.where(half, o[:span], o[span:]))
            high = l.astype(BF16).astype(F32)
            for n in range(2):
                for base, value in ((0, m), (32, high), (64, l - high)):
                    held = jnp.where(lanes == base + pair * 2 + n, value[n * span : (n + 1) * span], held)
        return held

    def attend_own(b):
        for copy in forwards[b]:
            copy.wait_recv()

        def keep(at, o):
            own_o[b, :, at] = o

        own_s[b] = attend(qown[b], b, span, keep)

    back = [[] for _ in range(nb)]

    def attend_other(b):
        for d in range(1, NX):
            q_out[b][NX - 1 - d].wait_recv()

            def give(at, o):
                out_o[d, b, :, at] = o.astype(BF16)

            out_o[d, b, :, inner:] = attend(qin[d, b], b, 0, give).astype(BF16)
            to = lax.rem(me + d * PAIR, R)
            back[b].append(go(out_o.at[d, b], in_o.at[NX - d, b], x_send.at[nb + b, d], x_recv.at[nb + b, d], row=to))

    attend_own(0)
    attend_other(0)
    for b in range(1, nb):
        for copy in forwards[b]:
            copy.wait_recv()
        attend_other(b)
    for b in range(1, nb):
        def keep(at, o, b=b):
            own_o[b, :, at] = o

        own_s[b] = attend(qown[b], b, span, keep)
    load_ow.wait()
    for b in range(nb):
        for copy in back[b]:
            copy.wait_recv()
        helds = [own_s[b]] + [in_o[d, b, :, inner:].astype(F32) for d in range(1, NX)]
        for pair in range(inner // (2 * HD)):
            at = slice(pair * 2 * HD, (pair + 1) * 2 * HD)

            def spread_of(held, base):
                one_of = held[:, base + pair * 2 : base + pair * 2 + 1]
                two_of = held[:, base + pair * 2 + 1 : base + pair * 2 + 2]
                return jnp.where(half, one_of, two_of)

            parts = [own_o[b, :, at]] + [in_o[d, b, :, at].astype(F32) for d in range(1, NX)]
            peaks = [spread_of(held, 0) for held in helds]
            top = functools.reduce(jnp.maximum, peaks)
            num, den = 0.0, 0.0
            for held, o, peak in zip(helds, parts, peaks):
                factor = jnp.exp(peak - top)
                num = num + o * factor
                den = den + (spread_of(held, 32) + spread_of(held, 64)) * factor
            attn[b, :, at] = (num / den).astype(BF16)
        hb = hfull[...].reshape(rows, nb, cols, channels)[:, b].reshape(span, channels)
        mixed_ref[b] = (hb + jnp.dot(attn[b], ow[...], preferred_element_type=F32)).astype(BF16)

    @pl.when(mc < C - 1)
    def _():
        to_right.wait_send()

    @pl.when(mc > 0)
    def _():
        to_left.wait_send()

    for k in range(1, C):
        for b in range(nb):
            each(k, b, lambda copy: copy.wait_send(), 1)
    for copy in started:
        copy.wait_send()


def body(
    latent,
    timestep,
    gn_gain,
    gn_bias,
    conv_weight,
    conv_bias,
    time_weight,
    ln_gain,
    q_weight,
    k_weight,
    v_weight,
    out_weight,
    stale_keys,
    stale_values,
):
    batch, rows, cols, channels = latent.shape
    inner = q_weight.shape[1]
    R, C = lax.axis_size("row"), lax.axis_size("col")
    NX = R // PAIR
    span = rows * cols
    wide = conv_weight.shape[3]
    count_all = span * R * C * (channels // GROUPS)
    vm = pl.BlockSpec(memory_space=pltpu.VMEM)
    hbm = pl.BlockSpec(memory_space=pl.ANY)
    dma = pltpu.SemaphoreType.DMA
    mixed, fresh_k, fresh_v = pl.pallas_call(
        functools.partial(kernel, (R, C, NX, rows, cols, channels, inner, count_all)),
        out_shape=(
            pltpu.VMEM((batch, span, channels), BF16),
            pltpu.VMEM((batch, span, inner), BF16),
            pltpu.VMEM((batch, span, inner), BF16),
        ),
        in_specs=[hbm] * 14,
        out_specs=(vm, vm, vm),
        scratch_shapes=[
            pltpu.SMEM(timestep.shape, jnp.int32),
            pltpu.VMEM((channels,), F32),
            pltpu.VMEM((channels,), F32),
            pltpu.VMEM((channels,), F32),
            pltpu.VMEM((channels,), F32),
            pltpu.VMEM((R, batch, rows, cols, channels), BF16),
            pltpu.VMEM((2, batch, rows, channels), BF16),
            pltpu.VMEM((R, 2, batch, rows, channels), BF16),
            pltpu.VMEM(time_weight.shape, BF16),
            pltpu.VMEM((3, R * rows + 2, batch * cols, channels), BF16),
            pltpu.VMEM((3, 3, wide, channels), BF16),
            pltpu.VMEM((channels, 3 * inner), BF16),
            pltpu.VMEM((inner, channels), BF16),
            pltpu.VMEM((R, 8, channels), F32),
            pltpu.VMEM((C, 8, channels), F32),
            pltpu.VMEM((R, batch * span, wide), BF16),
            pltpu.VMEM((R, batch * span, wide), BF16),
            pltpu.VMEM((batch * span, channels), F32),
            pltpu.VMEM((batch, (2 * C + 1) * span, inner), BF16),
            pltpu.VMEM((batch, (2 * C + 1) * span, inner), BF16),
            pltpu.VMEM((batch, span, inner), BF16),
            pltpu.VMEM((NX, batch, span, inner), BF16),
            pltpu.VMEM((batch, span, inner), F32),
            pltpu.VMEM((batch, span, 128), F32),
            pltpu.VMEM((NX, batch, span, inner + 128), BF16),
            pltpu.VMEM((NX, batch, span, inner + 128), BF16),
            pltpu.VMEM((batch, span, inner), BF16),
            dma((14,)),
            dma((batch + 3, R)),
            dma((batch + 3, R)),
            dma((1, C)),
            dma((1, C)),
            dma((C, 2, 2, batch)),
            dma((C, 2, 2, batch)),
            dma((2,)),
            dma((2,)),
            dma((2, batch)),
            dma((2, batch)),
            dma((2 * batch, NX)),
            dma((2 * batch, NX)),
        ],
        compiler_params=pltpu.CompilerParams(
            collective_id=0, has_side_effects=True, vmem_limit_bytes=56 * 1024 * 1024
        ),
    )(
        timestep,
        gn_gain,
        gn_bias,
        ln_gain,
        conv_bias,
        latent,
        time_weight,
        conv_weight.transpose(0, 1, 3, 2),
        q_weight,
        k_weight,
        v_weight,
        out_weight,
        stale_keys.reshape(batch, span, inner),
        stale_values.reshape(batch, span, inner),
    )
    held = (pltpu.with_memory_space_constraint(x, pltpu.VMEM) for x in (mixed, fresh_k, fresh_v))
    mixed, fresh_k, fresh_v = pl.pallas_call(
        finish,
        out_shape=tuple(jax.ShapeDtypeStruct(x.shape, x.dtype) for x in (mixed, fresh_k, fresh_v)),
        in_specs=[vm] * 3,
        out_specs=(hbm,) * 3,
        scratch_shapes=[dma((3,))],
    )(*held)
    return (
        mixed.reshape(batch, rows, cols, channels),
        fresh_k.reshape(batch, rows, cols, inner),
        fresh_v.reshape(batch, rows, cols, inner),
    )


def solution(mesh):
    placed = (
        P("parts", "row", "col", None),
        P("parts"),
        P(),
        P(),
        P(None, None, None, "row"),
        P(),
        P(),
        P(),
        P(),
        P(),
        P(),
        P(),
        P("parts", "row", "col", None),
        P("parts", "row", "col", None),
    )
    return jax.shard_map(
        body,
        mesh=mesh,
        in_specs=placed,
        out_specs=(
            P("parts", "row", "col", None),
            P("parts", "row", "col", None),
            P("parts", "row", "col", None),
        ),
        check_vma=False,
    )
```

```python
import functools

import jax
import jax.numpy as jnp
from jax import lax
from jax.experimental import pallas as pl
from jax.experimental.pallas import tpu as pltpu
from jax.sharding import PartitionSpec as P

HD = 64
GROUPS = 32
PAIR = 2
MESH = pl.DeviceIdType.MESH
F32 = jnp.float32
BF16 = jnp.bfloat16


def exact_dot(x, picks):
    total = None
    for _ in range(3):
        piece = x.astype(BF16)
        x = x - piece.astype(F32)
        part = jnp.dot(piece, picks, preferred_element_type=F32)
        total = part if total is None else total + part
    return total


def member(shape, group_dim, size):
    group = lax.broadcasted_iota(jnp.int32, shape, group_dim)
    first = group * size
    channel = lax.broadcasted_iota(jnp.int32, shape, 1 - group_dim)
    return jnp.where((channel >= first) & (channel < first + size), 1.0, 0.0).astype(BF16)


def finish(a, b, c, x, y, z, sem):
    copies = [pltpu.make_async_copy(p, q, sem.at[n]) for n, (p, q) in enumerate(((a, x), (b, y), (c, z)))]
    for copy in copies:
        copy.start()
    for copy in copies:
        copy.wait()


def fold(x, lines):
    count, wide = x.shape
    if lines == count:
        return x
    rest, more = wide % 128, lines - count
    turned = jnp.concatenate([x[n * more : (n + 1) * more, wide - rest :] for n in range(128 // rest)], axis=1)
    return jnp.concatenate([x[:, : wide - rest], turned], axis=0)


def unfold(x, count, wide):
    if x.shape[0] == count:
        return x
    rest = wide % 128
    back = [x[count:, n * rest : (n + 1) * rest] for n in range(128 // rest)]
    return jnp.concatenate([x[:count], jnp.concatenate(back, axis=0)], axis=1)


def silu(y):
    half = 0.5 * y
    return half + half * jnp.tanh(half)


def kernel(
    dims,
    t_hbm,
    gg_hbm,
    gb_hbm,
    lg_hbm,
    bias_hbm,
    lat_hbm,
    tw_hbm,
    cw_hbm,
    qw_hbm,
    kw_hbm,
    vw_hbm,
    ow_hbm,
    sk_hbm,
    sv_hbm,
    mixed_ref,
    fk_ref,
    fv_ref,
    t_ref,
    gg_ref,
    gb_ref,
    lg_ref,
    bias_ref,
    band,
    edges,
    halo,
    tw,
    acts,
    cw,
    qkvw,
    ow,
    rstats,
    cstats,
    hsend,
    hbuf,
    hfull,
    kbuf,
    vbuf,
    qall,
    own_o,
    own_s,
    out_o,
    in_o,
    attn,
    load_sem,
    row_send,
    row_recv,
    col_send,
    col_recv,
    hop_send,
    hop_recv,
    edge_send,
    edge_recv,
    side_send,
    side_recv,
    fwd_send,
    fwd_recv,
    x_send,
    x_recv,
    h_send,
    h_recv,
):
    R, C, NX, rows, cols, channels, inner, count_all = dims
    span = rows * cols
    wide = channels // R
    nb = 2
    me = lax.axis_index("row")
    mc = lax.axis_index("col")

    def remote(src, dst, send, recv, **where):
        return pltpu.make_async_remote_copy(
            src_ref=src, dst_ref=dst, send_sem=send, recv_sem=recv, device_id=where, device_id_type=MESH
        )

    def local(n, src, dst):
        return pltpu.make_async_copy(src, dst, load_sem.at[n])

    own_load = local(0, lat_hbm, band.at[me])
    own_load.start()
    barrier = pltpu.get_barrier_semaphore()
    near = C == 4
    has_left, has_right = mc > 0, mc < C - 1
    sides = ((has_left, lax.rem(mc + C - 1, C)), (has_right, lax.rem(mc + 1, C)))

    def greet(**where):
        pl.semaphore_signal(barrier, inc=1, device_id=where, device_id_type=MESH)

    for has, col in sides:

        @pl.when(has)
        def _(col=col):
            for d in range(0 if near else 1, R if near else NX):
                greet(row=lax.rem(me + d * (1 if near else PAIR), R), col=col)

    if not near:
        for d in range(1, C):
            greet(col=lax.rem(mc + d, C))
    for d in range(1, R):
        greet(row=lax.rem(me + d, R))
    beside = has_left.astype(jnp.int32) + has_right.astype(jnp.int32)
    expected = R - 1 + beside * R if near else R - 1 + C - 1 + beside * (NX - 1)
    load_k = local(1, sk_hbm, kbuf.at[:, 0:span])
    load_v = local(2, sv_hbm, vbuf.at[:, 0:span])
    load_t = [local(3, t_hbm, t_ref), local(4, bias_hbm, bias_ref), local(5, tw_hbm, tw)]
    load_gn = [local(6, gg_hbm, gg_ref), local(7, gb_hbm, gb_ref)]
    load_cw = local(8, cw_hbm, cw)
    load_q = [local(9, lg_hbm, lg_ref), local(10, qw_hbm, qkvw.at[:, 0:inner])]
    load_kv = [
        local(11, kw_hbm, qkvw.at[:, inner : 2 * inner]),
        local(12, vw_hbm, qkvw.at[:, 2 * inner : 3 * inner]),
    ]
    load_ow = local(13, ow_hbm, ow)
    for copy in [load_k, load_v] + load_t + load_gn + [load_cw] + load_q + load_kv + [load_ow]:
        copy.start()

    mate = me + 1 - 2 * lax.rem(me, PAIR)
    started = []

    def go(src, dst, send, recv, **where):
        copy = remote(src, dst, send, recv, **where)
        copy.start()
        started.append(copy)
        return copy

    own_load.wait()
    sums = [[], []]
    for b in range(nb):
        x = band[me, b].astype(F32)
        edges[0, b] = x[:, cols - 1, :].astype(BF16)
        edges[1, b] = x[:, 0, :].astype(BF16)
        flat = x.reshape(span, channels)
        sums[0].append(jnp.sum(flat, axis=0, keepdims=True))
        sums[1].append(jnp.sum(flat * flat, axis=0, keepdims=True))
    sums = jnp.concatenate(sums[0] + sums[1] + sums[0] + sums[1], axis=0)
    size = channels // GROUPS
    chip, core = me // PAIR, lax.rem(me, PAIR)
    rstats[0, 0] = exact_dot(sums * (1.0 / count_all), member((channels, 128), 1, size))
    if near:
        for n, (has, _) in enumerate(sides):

            @pl.when(jnp.logical_not(has))
            def _(n=n):
                rstats[1 + n] = jnp.zeros(rstats.shape[1:], F32)

    for n, (has, _) in enumerate(sides):

        @pl.when(jnp.logical_not(has))
        def _(n=n):
            halo[core, :, n] = jnp.zeros((NX,) + halo.shape[3:], BF16)


    pl.semaphore_wait(barrier, expected)

    def border(n, has, col):
        made = []
        if near:
            for d in range(R):
                made.append(
                    remote(
                        rstats.at[0, 0],
                        rstats.at[2 - n, d],
                        side_send.at[n, d],
                        side_recv.at[n, d],
                        row=lax.rem(me + d, R),
                        col=col,
                    )
                )
        for d in range(NX):
            made.append(
                remote(
                    edges.at[1 - n],
                    halo.at[core, chip, 1 - n],
                    edge_send.at[n, d],
                    edge_recv.at[n, d],
                    row=lax.rem(me + d * PAIR, R),
                    col=col,
                )
            )
        return made

    borders = [border(n, has, col) for n, (has, col) in enumerate(sides)]

    def beside_each(act, which):
        for n, (has, _) in enumerate(sides):

            @pl.when(has)
            def _(made=borders[which(n)]):
                for copy in made:
                    act(copy)

    row_stats = [
        go(rstats.at[0, 0], rstats.at[0, d], row_send.at[nb + 2, d], row_recv.at[nb + 2, d], row=lax.rem(me + R - d, R))
        for d in range(1, R)
    ]
    beside_each(lambda copy: copy.start(), lambda n: n)

    def spread(ref, n):
        cross = [
            go(ref, ref, row_send.at[n, k], row_recv.at[n, k], row=lax.rem(me + k * PAIR, R)) for k in range(1, NX)
        ]
        return [go(ref, ref, row_send.at[n, 0], row_recv.at[n, 0], row=mate)], cross

    def relay(cross, at, n):
        handed = []
        for k in range(1, NX):
            cross[k - 1].wait_recv()
            ref = at(lax.rem(me + R - k * PAIR, R))
            handed.append(go(ref, ref, row_send.at[n, NX - 1 + k], row_recv.at[n, NX - 1 + k], row=mate))
        return handed

    lat_out = [spread(band.at[me, b], b) for b in range(nb)]

    def through(k):
        return 1 if k == 3 else k - 1

    def hops(k, b):
        s = through(k)
        made = []
        for way, slot, dest, to, sends, takes in (
            (0, (C - s) % C, C - k, mc + k - s, (mc >= s) & (mc + k - s < C), mc >= k),
            (1, s, k, mc + s - k + C, (mc + s < C) & (mc + s >= k), mc + k < C),
        ):
            pair = [
                remote(
                    buf.at[b, slot * span : (slot + 1) * span],
                    buf.at[b, dest * span : (dest + 1) * span],
                    hop_send.at[k, n, way, b],
                    hop_recv.at[k, n, way, b],
                    col=lax.rem(to, C),
                )
                for n, buf in enumerate((kbuf, vbuf))
            ]
            made.append((pair, sends, takes))
        return made

    def each(k, b, act, which):
        for hop in hops(k, b):

            @pl.when(hop[which])
            def _(pair=hop[0]):
                for copy in pair:
                    act(copy)

    arrived = {(0, b) for b in range(nb)}

    def arrive(k, b):
        if (k, b) not in arrived:
            arrived.add((k, b))
            each(k, b, lambda copy: copy.wait_recv(), 2)

    def send_hop(k, b):
        arrive(through(k), b)
        each(k, b, lambda copy: copy.start(), 1)

    waiting = [(k, b) for k in range(4, C) for b in range(nb)]

    def advance(n):
        for _ in range(min(n, len(waiting))):
            send_hop(*waiting.pop(0))

    def pass_on(b):
        for k in (2, 3):
            if k < C:
                send_hop(k, b)

    load_k.wait()
    load_v.wait()
    if C > 1:
        send_hop(1, 0)

    half_t = tw.shape[0] // 2
    for copy in load_t:
        copy.wait()
    line = lax.broadcasted_iota(jnp.int32, (nb * cols, half_t), 0)
    when = jnp.where(line < cols, t_ref[0], t_ref[1]).astype(F32)
    place_t = lax.broadcasted_iota(jnp.int32, (nb * cols, half_t), 1).astype(F32)
    angles = when * jnp.exp(-jnp.log(jnp.full((1, 1), 10000.0, F32)) * place_t / half_t)
    temb = jnp.dot(
        jax.nn.silu(jnp.cos(angles)).astype(BF16), tw[0:half_t, :], preferred_element_type=F32
    ) + jnp.dot(jax.nn.silu(jnp.sin(angles)).astype(BF16), tw[half_t:, :], preferred_element_type=F32)
    temb = temb + bias_ref[...].reshape(1, channels)

    for copy in row_stats:
        copy.wait_recv()
    row_sum = functools.reduce(lambda p, q: p + q, [rstats[0, d] for d in range(R)])
    beside_each(lambda copy: copy.wait_recv(), lambda n: 1 - n)
    if near:
        left_sum = functools.reduce(lambda p, q: p + q, [rstats[1, d] for d in range(R)])
        right_sum = functools.reduce(lambda p, q: p + q, [rstats[2, d] for d in range(R)])
        cstats[0] = row_sum + jnp.where(mc < 2, left_sum, right_sum)
        col_stats = [go(cstats.at[0], cstats.at[1], col_send.at[0, 0], col_recv.at[0, 0], col=lax.rem(mc + 2, C))]
    else:
        cstats[0] = row_sum
        col_stats = [
            go(cstats.at[0], cstats.at[C - d], col_send.at[0, d], col_recv.at[0, d], col=lax.rem(mc + d, C))
            for d in range(1, C)
        ]
    handed = [go(halo.at[core], halo.at[core], row_send.at[nb, 0], row_recv.at[nb, 0], row=mate)]
    for b in range(1, nb):
        if C > 1:
            send_hop(1, b)
    for t in range(3):
        acts[t, 0] = jnp.zeros(acts.shape[2:], BF16)
        acts[t, R * rows + 1] = jnp.zeros(acts.shape[2:], BF16)
    pass_on(0)
    for b in range(nb):
        handed += relay(lat_out[b][1], lambda p, b=b: band.at[p, b], b)
    for b in range(1, nb):
        pass_on(b)
    for copy in load_gn:
        copy.wait()
    for b in range(nb):
        lat_out[b][0][0].wait_recv()
    for copy in col_stats:
        copy.wait_recv()
    if near:
        total = row_sum + left_sum + right_sum + cstats[1]
    else:
        total = functools.reduce(lambda p, q: p + q, [cstats[d] for d in range(C)])
    middle = total[0:nb]
    inverse = lax.rsqrt(total[nb : 2 * nb] - middle * middle + 1e-05)
    spread_out = exact_dot(jnp.concatenate([middle, inverse] * 2, axis=0), member((128, channels), 0, size))
    gain = gg_ref[...].reshape(1, channels)
    scale = [spread_out[nb + b : nb + b + 1] * gain for b in range(nb)]
    shift = [gb_ref[...].reshape(1, channels) - spread_out[b : b + 1] * scale[b] for b in range(nb)]
    for copy in handed:
        copy.wait_recv()

    def activate(x, b):
        return silu(x.astype(F32) * scale[b] + shift[b])

    for j in range(NX):
        at = lax.rem(chip + j, NX) * PAIR + core
        base = jnp.concatenate([band[at, b].astype(F32) for b in range(nb)], axis=1)
        hfull[j] = (base + temb[None]).reshape(nb * span, channels)
    place = lax.broadcasted_iota(jnp.int32, (rows, cols, channels), 1)
    for r in range(R):
        tap = [[], [], []]
        for b in range(nb):
            a = activate(band[r, b], b)
            left = jnp.where(mc > 0, activate(halo[r % PAIR, r // PAIR, 0, b], b), 0.0)
            right = jnp.where(mc < C - 1, activate(halo[r % PAIR, r // PAIR, 1, b], b), 0.0)
            tap[0].append(jnp.where(place == 0, left[:, None, :], pltpu.roll(a, 1, 1)))
            tap[1].append(a)
            tap[2].append(jnp.where(place == cols - 1, right[:, None, :], pltpu.roll(a, cols - 1, 1)))
        for t in range(3):
            acts[t, 1 + r * rows : 1 + (r + 1) * rows] = jnp.concatenate(tap[t], axis=1).astype(BF16)
    load_cw.wait()
    lines = hsend.shape[2]
    h_out = {}
    for k in range(NX):
        owner = lax.rem(chip + k, NX)
        top = owner * (PAIR * rows)
        acc = None
        for across in range(3):
            for down in range(3):
                part = lax.dot_general(
                    acts[across, pl.ds(top + down, PAIR * rows)].reshape(PAIR * rows * nb * cols, channels),
                    cw[down, across],
                    (((1,), (1,)), ((), ())),
                    preferred_element_type=F32,
                )
                acc = part if acc is None else acc + part
        acc = acc.reshape(PAIR, nb * span, wide)
        for c in range(PAIR):
            hsend[c, owner] = fold(acc[c], lines).astype(BF16)
        for far in list(range(1, NX)) + [0]:
            for turn in range(PAIR):
                if far or turn:
                    c = lax.rem(core + turn, PAIR)
                    h_out[k, far, turn] = go(
                        hsend.at[c, owner],
                        hbuf.at[me, owner],
                        h_send.at[k, far, turn],
                        h_recv.at[k, far, turn],
                        row=lax.rem(chip + far, NX) * PAIR + c,
                    )
        hbuf[me, owner] = hsend[core, owner]
        advance(1)
    advance(len(waiting))

    def normed_of(j):
        for (k, far, turn), copy in h_out.items():
            if (k - far) % NX == j:
                copy.wait_recv()
        owner = lax.rem(chip + j, NX)
        h = hfull[j] + jnp.concatenate([unfold(hbuf[r, owner].astype(F32), nb * span, wide) for r in range(R)], axis=1)
        h = h.astype(BF16).astype(F32)
        if j == 0:
            hfull[0] = h
        centre = h - jnp.mean(h, axis=1, keepdims=True)
        spread_h = jnp.mean(centre * centre, axis=1, keepdims=True)
        return (centre * lax.rsqrt(spread_h + 1e-05) * lg_ref[...].reshape(1, channels)).astype(BF16)

    def project(normed, first, last):
        out = jnp.dot(normed, qkvw[:, first * inner : last * inner], preferred_element_type=F32)
        return out.reshape(rows, nb, cols, (last - first) * inner)

    def queries(j, whole):
        for b in range(nb):
            qall[j, b] = (whole[:, b, :, 0:inner].reshape(span, inner) * (1.0 / HD**0.5)).astype(BF16)

    forwards = []

    def forward(b):
        for k in range(1, C):
            arrive(k, b)
        forwards.append(
            [
                go(buf.at[b, 0 : C * span], buf.at[b, C * span : 2 * C * span], fwd_send.at[n, b], fwd_recv.at[n, b], row=mate)
                for n, buf in enumerate((kbuf, vbuf))
            ]
        )

    for b in range(nb):
        forward(b)
    for copy in load_q:
        copy.wait()
    for j in range(1, NX):
        queries(j, project(normed_of(j), 0, 1))

    half = lax.broadcasted_iota(jnp.int32, (span, 2 * HD), 1) < HD
    lanes = lax.broadcasted_iota(jnp.int32, (span, 128), 1)
    zero = jnp.zeros((span, 2 * HD), BF16)

    def attend(q, b, start, o_store):
        held = jnp.zeros((span, 128), F32)
        for pair in range(inner // (2 * HD)):
            at = slice(pair * 2 * HD, (pair + 1) * 2 * HD)
            q2 = q[:, at]
            q2 = jnp.concatenate([jnp.where(half, q2, zero), jnp.where(half, zero, q2)], axis=0)
            s = lax.dot_general(
                q2, kbuf[b, start : start + 2 * C * span, at], (((1,), (1,)), ((), ())), preferred_element_type=F32
            )
            m = jnp.max(s, axis=1, keepdims=True).astype(BF16).astype(F32)
            p = jnp.exp(s - m)
            l = jnp.sum(p, axis=1, keepdims=True)
            o = jnp.dot(p.astype(BF16), vbuf[b, start : start + 2 * C * span, at], preferred_element_type=F32)
            o_store(at, jnp.where(half, o[:span], o[span:]))
            high = l.astype(BF16).astype(F32)
            for n in range(2):
                for base, value in ((0, m), (32, high), (64, l - high)):
                    held = jnp.where(lanes == base + pair * 2 + n, value[n * span : (n + 1) * span], held)
        return held

    back = []
    for b in range(nb):
        for copy in forwards[b]:
            copy.wait_recv()
        sent = []
        for j in range(1, NX):

            def give(at, o):
                out_o[j, b, :, at] = o.astype(BF16)

            out_o[j, b, :, inner:] = attend(qall[j, b], b, 0, give).astype(BF16)
            to = lax.rem(me + j * PAIR, R)
            sent.append(go(out_o.at[j, b], in_o.at[NX - j, b], x_send.at[b, j], x_recv.at[b, j], row=to))
        back.append(sent)
    for copy in load_kv:
        copy.wait()
    fresh = project(normed_of(0), 0, 3)
    queries(0, fresh)
    for b in range(nb):
        k = fresh[:, b, :, inner : 2 * inner].reshape(span, inner).astype(BF16)
        v = fresh[:, b, :, 2 * inner :].reshape(span, inner).astype(BF16)
        kbuf[b, 2 * C * span :] = k
        vbuf[b, 2 * C * span :] = v
        fk_ref[b] = k
        fv_ref[b] = v
    for b in range(nb):

        def keep(at, o):
            own_o[b, :, at] = o

        own_s[b] = attend(qall[0, b], b, span, keep)
    load_ow.wait()
    for b in range(nb):
        for copy in back[b]:
            copy.wait_recv()
        helds = [own_s[b]] + [in_o[d, b, :, inner:].astype(F32) for d in range(1, NX)]
        for pair in range(inner // (2 * HD)):
            at = slice(pair * 2 * HD, (pair + 1) * 2 * HD)

            def spread_of(held, base):
                one_of = held[:, base + pair * 2 : base + pair * 2 + 1]
                two_of = held[:, base + pair * 2 + 1 : base + pair * 2 + 2]
                return jnp.where(half, one_of, two_of)

            parts = [own_o[b, :, at]] + [in_o[d, b, :, at].astype(F32) for d in range(1, NX)]
            peaks = [spread_of(held, 0) for held in helds]
            top = functools.reduce(jnp.maximum, peaks)
            num, den = 0.0, 0.0
            for held, o, peak in zip(helds, parts, peaks):
                factor = jnp.exp(peak - top)
                num = num + o * factor
                den = den + (spread_of(held, 32) + spread_of(held, 64)) * factor
            attn[b, :, at] = (num / den).astype(BF16)
        hb = hfull[0].reshape(rows, nb, cols, channels)[:, b].reshape(span, channels)
        mixed_ref[b] = (hb + jnp.dot(attn[b], ow[...], preferred_element_type=F32)).astype(BF16)

    beside_each(lambda copy: copy.wait_send(), lambda n: n)
    for k in range(1, C):
        for b in range(nb):
            each(k, b, lambda copy: copy.wait_send(), 1)
    for copy in started:
        copy.wait_send()


def body(
    latent,
    timestep,
    gn_gain,
    gn_bias,
    conv_weight,
    conv_bias,
    time_weight,
    ln_gain,
    q_weight,
    k_weight,
    v_weight,
    out_weight,
    stale_keys,
    stale_values,
):
    batch, rows, cols, channels = latent.shape
    inner = q_weight.shape[1]
    R, C = lax.axis_size("row"), lax.axis_size("col")
    NX = R // PAIR
    span = rows * cols
    wide = conv_weight.shape[3]
    count_all = span * R * C * (channels // GROUPS)
    rest = wide % 128
    if wide // 128 == 1 and rest and 128 % rest == 0 and batch * span * rest % (16 * 128) == 0:
        block = (batch * span + batch * span * rest // 128, 128)
    else:
        block = (batch * span, wide)
    vm = pl.BlockSpec(memory_space=pltpu.VMEM)
    hbm = pl.BlockSpec(memory_space=pl.ANY)
    dma = pltpu.SemaphoreType.DMA
    mixed, fresh_k, fresh_v = pl.pallas_call(
        functools.partial(kernel, (R, C, NX, rows, cols, channels, inner, count_all)),
        out_shape=(
            pltpu.VMEM((batch, span, channels), BF16),
            pltpu.VMEM((batch, span, inner), BF16),
            pltpu.VMEM((batch, span, inner), BF16),
        ),
        in_specs=[hbm] * 14,
        out_specs=(vm, vm, vm),
        scratch_shapes=[
            pltpu.SMEM(timestep.shape, jnp.int32),
            pltpu.VMEM((channels,), F32),
            pltpu.VMEM((channels,), F32),
            pltpu.VMEM((channels,), F32),
            pltpu.VMEM((channels,), F32),
            pltpu.VMEM((R, batch, rows, cols, channels), BF16),
            pltpu.VMEM((2, batch, rows, channels), BF16),
            pltpu.VMEM((PAIR, NX, 2, batch, rows, channels), BF16),
            pltpu.VMEM(time_weight.shape, BF16),
            pltpu.VMEM((3, R * rows + 2, batch * cols, channels), BF16),
            pltpu.VMEM((3, 3, wide, channels), BF16),
            pltpu.VMEM((channels, 3 * inner), BF16),
            pltpu.VMEM((inner, channels), BF16),
            pltpu.VMEM((3, R, 8, 128), F32),
            pltpu.VMEM((C, 8, 128), F32),
            pltpu.VMEM((PAIR, NX) + block, BF16),
            pltpu.VMEM((R, NX) + block, BF16),
            pltpu.VMEM((NX, batch * span, channels), F32),
            pltpu.VMEM((batch, (2 * C + 1) * span, inner), BF16),
            pltpu.VMEM((batch, (2 * C + 1) * span, inner), BF16),
            pltpu.VMEM((NX, batch, span, inner), BF16),
            pltpu.VMEM((batch, span, inner), F32),
            pltpu.VMEM((batch, span, 128), F32),
            pltpu.VMEM((NX, batch, span, inner + 128), BF16),
            pltpu.VMEM((NX, batch, span, inner + 128), BF16),
            pltpu.VMEM((batch, span, inner), BF16),
            dma((14,)),
            dma((batch + 3, R)),
            dma((batch + 3, R)),
            dma((1, C)),
            dma((1, C)),
            dma((C, 2, 2, batch)),
            dma((C, 2, 2, batch)),
            dma((2, NX)),
            dma((2, NX)),
            dma((2, R)),
            dma((2, R)),
            dma((2, batch)),
            dma((2, batch)),
            dma((batch, NX)),
            dma((batch, NX)),
            dma((NX, NX, PAIR)),
            dma((NX, NX, PAIR)),
        ],
        compiler_params=pltpu.CompilerParams(
            collective_id=0, has_side_effects=True, vmem_limit_bytes=56 * 1024 * 1024
        ),
    )(
        timestep,
        gn_gain,
        gn_bias,
        ln_gain,
        conv_bias,
        latent,
        time_weight,
        conv_weight.transpose(0, 1, 3, 2),
        q_weight,
        k_weight,
        v_weight,
        out_weight,
        stale_keys.reshape(batch, span, inner),
        stale_values.reshape(batch, span, inner),
    )
    held = (pltpu.with_memory_space_constraint(x, pltpu.VMEM) for x in (mixed, fresh_k, fresh_v))
    mixed, fresh_k, fresh_v = pl.pallas_call(
        finish,
        out_shape=tuple(jax.ShapeDtypeStruct(x.shape, x.dtype) for x in (mixed, fresh_k, fresh_v)),
        in_specs=[vm] * 3,
        out_specs=(hbm,) * 3,
        scratch_shapes=[dma((3,))],
    )(*held)
    return (
        mixed.reshape(batch, rows, cols, channels),
        fresh_k.reshape(batch, rows, cols, inner),
        fresh_v.reshape(batch, rows, cols, inner),
    )


def solution(mesh):
    placed = (
        P("parts", "row", "col", None),
        P("parts"),
        P(),
        P(),
        P(None, None, None, "row"),
        P(),
        P(),
        P(),
        P(),
        P(),
        P(),
        P(),
        P("parts", "row", "col", None),
        P("parts", "row", "col", None),
    )
    return jax.shard_map(
        body,
        mesh=mesh,
        in_specs=placed,
        out_specs=(
            P("parts", "row", "col", None),
            P("parts", "row", "col", None),
            P("parts", "row", "col", None),
        ),
        check_vma=False,
    )
```

```python
import functools

import jax
import jax.numpy as jnp
from jax import lax
from jax.experimental import pallas as pl
from jax.experimental.pallas import tpu as pltpu
from jax.sharding import PartitionSpec as P

HD = 64
GROUPS = 32
PAIR = 2
MESH = pl.DeviceIdType.MESH
F32 = jnp.float32
BF16 = jnp.bfloat16


def exact_dot(x, picks):
    total = None
    for _ in range(3):
        piece = x.astype(BF16)
        x = x - piece.astype(F32)
        part = jnp.dot(piece, picks, preferred_element_type=F32)
        total = part if total is None else total + part
    return total


def member(shape, group_dim, size):
    group = lax.broadcasted_iota(jnp.int32, shape, group_dim)
    first = group * size
    channel = lax.broadcasted_iota(jnp.int32, shape, 1 - group_dim)
    return jnp.where((channel >= first) & (channel < first + size), 1.0, 0.0).astype(BF16)


def finish(a, b, c, x, y, z, sem):
    copies = [pltpu.make_async_copy(p, q, sem.at[n]) for n, (p, q) in enumerate(((a, x), (b, y), (c, z)))]
    for copy in copies:
        copy.start()
    for copy in copies:
        copy.wait()


def fold(x, lines):
    count, wide = x.shape
    if lines == count:
        return x
    rest, more = wide % 128, lines - count
    turned = jnp.concatenate([x[n * more : (n + 1) * more, wide - rest :] for n in range(128 // rest)], axis=1)
    return jnp.concatenate([x[:, : wide - rest], turned], axis=0)


def unfold(x, count, wide):
    if x.shape[0] == count:
        return x
    rest = wide % 128
    back = [x[count:, n * rest : (n + 1) * rest] for n in range(128 // rest)]
    return jnp.concatenate([x[:count], jnp.concatenate(back, axis=0)], axis=1)


def silu(y):
    half = 0.5 * y
    return half + half * jnp.tanh(half)


def kernel(
    dims,
    t_hbm,
    gg_hbm,
    gb_hbm,
    lg_hbm,
    bias_hbm,
    lat_hbm,
    tw_hbm,
    cw_hbm,
    qw_hbm,
    kw_hbm,
    vw_hbm,
    ow_hbm,
    sk_hbm,
    sv_hbm,
    mixed_ref,
    fk_ref,
    fv_ref,
    t_ref,
    gg_ref,
    gb_ref,
    lg_ref,
    bias_ref,
    band,
    edges,
    halo,
    tw,
    acts,
    cw,
    qkvw,
    ow,
    rstats,
    cstats,
    hsend,
    hbuf,
    hfull,
    kbuf,
    vbuf,
    qall,
    own_o,
    own_s,
    out_o,
    in_o,
    attn,
    load_sem,
    row_send,
    row_recv,
    col_send,
    col_recv,
    hop_send,
    hop_recv,
    edge_send,
    edge_recv,
    side_send,
    side_recv,
    fwd_send,
    fwd_recv,
    x_send,
    x_recv,
    h_send,
    h_recv,
):
    R, C, NX, rows, cols, channels, inner, count_all = dims
    span = rows * cols
    wide = channels // R
    nb = 2
    me = lax.axis_index("row")
    mc = lax.axis_index("col")

    def remote(src, dst, send, recv, **where):
        return pltpu.make_async_remote_copy(
            src_ref=src, dst_ref=dst, send_sem=send, recv_sem=recv, device_id=where, device_id_type=MESH
        )

    def local(n, src, dst):
        return pltpu.make_async_copy(src, dst, load_sem.at[n])

    own_load = local(0, lat_hbm, band.at[me])
    own_load.start()
    barrier = pltpu.get_barrier_semaphore()
    near = C == 4
    has_left, has_right = mc > 0, mc < C - 1
    sides = ((has_left, lax.rem(mc + C - 1, C)), (has_right, lax.rem(mc + 1, C)))

    def greet(**where):
        pl.semaphore_signal(barrier, inc=1, device_id=where, device_id_type=MESH)

    for has, col in sides:

        @pl.when(has)
        def _(col=col):
            for d in range(0 if near else 1, R if near else NX):
                greet(row=lax.rem(me + d * (1 if near else PAIR), R), col=col)

    if not near:
        for d in range(1, C):
            greet(col=lax.rem(mc + d, C))
    for d in range(1, R):
        greet(row=lax.rem(me + d, R))
    beside = has_left.astype(jnp.int32) + has_right.astype(jnp.int32)
    expected = R - 1 + beside * R if near else R - 1 + C - 1 + beside * (NX - 1)
    load_k = local(1, sk_hbm, kbuf.at[:, 0:span])
    load_v = local(2, sv_hbm, vbuf.at[:, 0:span])
    load_t = [local(3, t_hbm, t_ref), local(4, bias_hbm, bias_ref), local(5, tw_hbm, tw)]
    load_gn = [local(6, gg_hbm, gg_ref), local(7, gb_hbm, gb_ref)]
    load_cw = local(8, cw_hbm, cw)
    load_q = [local(9, lg_hbm, lg_ref), local(10, qw_hbm, qkvw.at[:, 0:inner])]
    load_kv = [
        local(11, kw_hbm, qkvw.at[:, inner : 2 * inner]),
        local(12, vw_hbm, qkvw.at[:, 2 * inner : 3 * inner]),
    ]
    load_ow = local(13, ow_hbm, ow)
    for copy in [load_k, load_v] + load_t + load_gn + [load_cw] + load_q + load_kv + [load_ow]:
        copy.start()

    mate = me + 1 - 2 * lax.rem(me, PAIR)
    started = []

    def go(src, dst, send, recv, **where):
        copy = remote(src, dst, send, recv, **where)
        copy.start()
        started.append(copy)
        return copy

    own_load.wait()
    sums = [[], []]
    for b in range(nb):
        x = band[me, b].astype(F32)
        edges[0, b] = x[:, cols - 1, :].astype(BF16)
        edges[1, b] = x[:, 0, :].astype(BF16)
        flat = x.reshape(span, channels)
        sums[0].append(jnp.sum(flat, axis=0, keepdims=True))
        sums[1].append(jnp.sum(flat * flat, axis=0, keepdims=True))
    sums = jnp.concatenate(sums[0] + sums[1] + sums[0] + sums[1], axis=0)
    size = channels // GROUPS
    chip, core = me // PAIR, lax.rem(me, PAIR)
    rstats[0, 0] = exact_dot(sums * (1.0 / count_all), member((channels, 128), 1, size))
    if near:
        for n, (has, _) in enumerate(sides):

            @pl.when(jnp.logical_not(has))
            def _(n=n):
                rstats[1 + n] = jnp.zeros(rstats.shape[1:], F32)

    for n, (has, _) in enumerate(sides):

        @pl.when(jnp.logical_not(has))
        def _(n=n):
            halo[core, :, n] = jnp.zeros((NX,) + halo.shape[3:], BF16)


    pl.semaphore_wait(barrier, expected)

    def border(n, has, col):
        made = []
        if near:
            for d in range(R):
                made.append(
                    remote(
                        rstats.at[0, 0],
                        rstats.at[2 - n, d],
                        side_send.at[n, d],
                        side_recv.at[n, d],
                        row=lax.rem(me + d, R),
                        col=col,
                    )
                )
        for d in range(NX):
            made.append(
                remote(
                    edges.at[1 - n],
                    halo.at[core, chip, 1 - n],
                    edge_send.at[n, d],
                    edge_recv.at[n, d],
                    row=lax.rem(me + d * PAIR, R),
                    col=col,
                )
            )
        return made

    borders = [border(n, has, col) for n, (has, col) in enumerate(sides)]

    def beside_each(act, which):
        for n, (has, _) in enumerate(sides):

            @pl.when(has)
            def _(made=borders[which(n)]):
                for copy in made:
                    act(copy)

    row_stats = [
        go(rstats.at[0, 0], rstats.at[0, d], row_send.at[nb + 2, d], row_recv.at[nb + 2, d], row=lax.rem(me + R - d, R))
        for d in range(1, R)
    ]
    beside_each(lambda copy: copy.start(), lambda n: n)

    def spread(ref, n):
        cross = [
            go(ref, ref, row_send.at[n, k], row_recv.at[n, k], row=lax.rem(me + k * PAIR, R)) for k in range(1, NX)
        ]
        return [go(ref, ref, row_send.at[n, 0], row_recv.at[n, 0], row=mate)], cross

    def relay(cross, at, n):
        handed = []
        for k in range(1, NX):
            cross[k - 1].wait_recv()
            ref = at(lax.rem(me + R - k * PAIR, R))
            handed.append(go(ref, ref, row_send.at[n, NX - 1 + k], row_recv.at[n, NX - 1 + k], row=mate))
        return handed

    lat_out = [spread(band.at[me, b], b) for b in range(nb)]

    pieces = [(b, n) for b in range(nb) for n in range(2)]

    def hops(k, part):
        b, n = part
        buf = (kbuf, vbuf)[n]
        made = []
        for way, slot, dest, to, sends, takes in (
            (0, (C - k + 1) % C, C - k, mc + 1, (mc >= k - 1) & (mc < C - 1), mc >= k),
            (1, k - 1, k, mc + C - 1, (mc <= C - k) & (mc > 0), mc <= C - 1 - k),
        ):
            copy = remote(
                buf.at[b, slot * span : (slot + 1) * span],
                buf.at[b, dest * span : (dest + 1) * span],
                hop_send.at[k, n, way, b],
                hop_recv.at[k, n, way, b],
                col=lax.rem(to, C),
            )
            made.append((copy, sends, takes))
        return made

    def each(k, part, act, which):
        for hop in hops(k, part):

            @pl.when(hop[which])
            def _(copy=hop[0]):
                act(copy)

    def send_hop(k, part):
        if k > 1:
            each(k - 1, part, lambda copy: copy.wait_recv(), 2)
        if k < C:
            each(k, part, lambda copy: copy.start(), 1)

    waiting = [(k, part) for k in range(2, C) for part in pieces]

    def advance(n):
        for _ in range(min(n, len(waiting))):
            send_hop(*waiting.pop(0))

    load_k.wait()
    load_v.wait()
    for part in pieces:
        send_hop(1, part)

    half_t = tw.shape[0] // 2
    for copy in load_t:
        copy.wait()
    line = lax.broadcasted_iota(jnp.int32, (nb * cols, half_t), 0)
    when = jnp.where(line < cols, t_ref[0], t_ref[1]).astype(F32)
    place_t = lax.broadcasted_iota(jnp.int32, (nb * cols, half_t), 1).astype(F32)
    angles = when * jnp.exp(-jnp.log(jnp.full((1, 1), 10000.0, F32)) * place_t / half_t)
    temb = jnp.dot(
        jax.nn.silu(jnp.cos(angles)).astype(BF16), tw[0:half_t, :], preferred_element_type=F32
    ) + jnp.dot(jax.nn.silu(jnp.sin(angles)).astype(BF16), tw[half_t:, :], preferred_element_type=F32)
    temb = temb + bias_ref[...].reshape(1, channels)

    for copy in row_stats:
        copy.wait_recv()
    row_sum = functools.reduce(lambda p, q: p + q, [rstats[0, d] for d in range(R)])
    beside_each(lambda copy: copy.wait_recv(), lambda n: 1 - n)
    if near:
        left_sum = functools.reduce(lambda p, q: p + q, [rstats[1, d] for d in range(R)])
        right_sum = functools.reduce(lambda p, q: p + q, [rstats[2, d] for d in range(R)])
        cstats[0] = row_sum + jnp.where(mc < 2, left_sum, right_sum)
        col_stats = [go(cstats.at[0], cstats.at[1], col_send.at[0, 0], col_recv.at[0, 0], col=lax.rem(mc + 2, C))]
    else:
        cstats[0] = row_sum
        col_stats = [
            go(cstats.at[0], cstats.at[C - d], col_send.at[0, d], col_recv.at[0, d], col=lax.rem(mc + d, C))
            for d in range(1, C)
        ]
    handed = [go(halo.at[core], halo.at[core], row_send.at[nb, 0], row_recv.at[nb, 0], row=mate)]
    for t in range(3):
        acts[t, 0] = jnp.zeros(acts.shape[2:], BF16)
        acts[t, R * rows + 1] = jnp.zeros(acts.shape[2:], BF16)
    advance(2)
    for b in range(nb):
        handed += relay(lat_out[b][1], lambda p, b=b: band.at[p, b], b)
        advance(1)
    for copy in load_gn:
        copy.wait()
    for b in range(nb):
        lat_out[b][0][0].wait_recv()
    for copy in col_stats:
        copy.wait_recv()
    if near:
        total = row_sum + left_sum + right_sum + cstats[1]
    else:
        total = functools.reduce(lambda p, q: p + q, [cstats[d] for d in range(C)])
    middle = total[0:nb]
    inverse = lax.rsqrt(total[nb : 2 * nb] - middle * middle + 1e-05)
    spread_out = exact_dot(jnp.concatenate([middle, inverse] * 2, axis=0), member((128, channels), 0, size))
    gain = gg_ref[...].reshape(1, channels)
    scale = [spread_out[nb + b : nb + b + 1] * gain for b in range(nb)]
    shift = [gb_ref[...].reshape(1, channels) - spread_out[b : b + 1] * scale[b] for b in range(nb)]
    for copy in handed:
        copy.wait_recv()

    def activate(x, b):
        return silu(x.astype(F32) * scale[b] + shift[b])

    for j in range(NX):
        at = lax.rem(chip + j, NX) * PAIR + core
        base = jnp.concatenate([band[at, b].astype(F32) for b in range(nb)], axis=1)
        hfull[j] = (base + temb[None]).reshape(nb * span, channels)
    place = lax.broadcasted_iota(jnp.int32, (rows, cols, channels), 1)
    for r in range(R):
        tap = [[], [], []]
        for b in range(nb):
            a = activate(band[r, b], b)
            left = jnp.where(mc > 0, activate(halo[r % PAIR, r // PAIR, 0, b], b), 0.0)
            right = jnp.where(mc < C - 1, activate(halo[r % PAIR, r // PAIR, 1, b], b), 0.0)
            tap[0].append(jnp.where(place == 0, left[:, None, :], pltpu.roll(a, 1, 1)))
            tap[1].append(a)
            tap[2].append(jnp.where(place == cols - 1, right[:, None, :], pltpu.roll(a, cols - 1, 1)))
        for t in range(3):
            acts[t, 1 + r * rows : 1 + (r + 1) * rows] = jnp.concatenate(tap[t], axis=1).astype(BF16)
    advance(1)
    load_cw.wait()
    lines = hsend.shape[2]
    h_out = {}
    for k in range(NX):
        owner = lax.rem(chip + k, NX)
        top = owner * (PAIR * rows)
        acc = None
        for across in range(3):
            for down in range(3):
                part = lax.dot_general(
                    acts[across, pl.ds(top + down, PAIR * rows)].reshape(PAIR * rows * nb * cols, channels),
                    cw[down, across],
                    (((1,), (1,)), ((), ())),
                    preferred_element_type=F32,
                )
                acc = part if acc is None else acc + part
        acc = acc.reshape(PAIR, nb * span, wide)
        for c in range(PAIR):
            hsend[c, owner] = fold(acc[c], lines).astype(BF16)
        for far in list(range(1, NX)) + [0]:
            for turn in range(PAIR):
                if far or turn:
                    c = lax.rem(core + turn, PAIR)
                    h_out[k, far, turn] = go(
                        hsend.at[c, owner],
                        hbuf.at[me, owner],
                        h_send.at[k, far, turn],
                        h_recv.at[k, far, turn],
                        row=lax.rem(chip + far, NX) * PAIR + c,
                    )
        hbuf[me, owner] = hsend[core, owner]
        advance(2)
    advance(len(waiting))

    def normed_of(j):
        for (k, far, turn), copy in h_out.items():
            if (k - far) % NX == j:
                copy.wait_recv()
        owner = lax.rem(chip + j, NX)
        h = hfull[j] + jnp.concatenate([unfold(hbuf[r, owner].astype(F32), nb * span, wide) for r in range(R)], axis=1)
        h = h.astype(BF16).astype(F32)
        if j == 0:
            hfull[0] = h
        centre = h - jnp.mean(h, axis=1, keepdims=True)
        spread_h = jnp.mean(centre * centre, axis=1, keepdims=True)
        return (centre * lax.rsqrt(spread_h + 1e-05) * lg_ref[...].reshape(1, channels)).astype(BF16)

    def project(normed, first, last):
        out = jnp.dot(normed, qkvw[:, first * inner : last * inner], preferred_element_type=F32)
        return out.reshape(rows, nb, cols, (last - first) * inner)

    def queries(j, whole):
        for b in range(nb):
            qall[j, b] = (whole[:, b, :, 0:inner].reshape(span, inner) * (1.0 / HD**0.5)).astype(BF16)

    forwards = {}
    for part in pieces:
        b, n = part
        buf = (kbuf, vbuf)[n]
        send_hop(C, part)
        forwards[part] = go(
            buf.at[b, 0 : C * span], buf.at[b, C * span : 2 * C * span], fwd_send.at[n, b], fwd_recv.at[n, b], row=mate
        )
    for copy in load_q:
        copy.wait()
    for j in range(1, NX):
        queries(j, project(normed_of(j), 0, 1))

    half = lax.broadcasted_iota(jnp.int32, (span, 2 * HD), 1) < HD
    lanes = lax.broadcasted_iota(jnp.int32, (span, 128), 1)
    zero = jnp.zeros((span, 2 * HD), BF16)

    def attend(q, b, start, o_store):
        held = jnp.zeros((span, 128), F32)
        for pair in range(inner // (2 * HD)):
            at = slice(pair * 2 * HD, (pair + 1) * 2 * HD)
            q2 = q[:, at]
            q2 = jnp.concatenate([jnp.where(half, q2, zero), jnp.where(half, zero, q2)], axis=0)
            s = lax.dot_general(
                q2, kbuf[b, start : start + 2 * C * span, at], (((1,), (1,)), ((), ())), preferred_element_type=F32
            )
            m = jnp.max(s, axis=1, keepdims=True).astype(BF16).astype(F32)
            p = jnp.exp(s - m)
            l = jnp.sum(p, axis=1, keepdims=True)
            o = jnp.dot(p.astype(BF16), vbuf[b, start : start + 2 * C * span, at], preferred_element_type=F32)
            o_store(at, jnp.where(half, o[:span], o[span:]))
            high = l.astype(BF16).astype(F32)
            for n in range(2):
                for base, value in ((0, m), (32, high), (64, l - high)):
                    held = jnp.where(lanes == base + pair * 2 + n, value[n * span : (n + 1) * span], held)
        return held

    back = []
    for b in range(nb):
        for n in range(2):
            forwards[b, n].wait_recv()
        sent = []
        for j in range(1, NX):

            def give(at, o):
                out_o[j, b, :, at] = o.astype(BF16)

            out_o[j, b, :, inner:] = attend(qall[j, b], b, 0, give).astype(BF16)
            to = lax.rem(me + j * PAIR, R)
            sent.append(go(out_o.at[j, b], in_o.at[NX - j, b], x_send.at[b, j], x_recv.at[b, j], row=to))
        back.append(sent)
    for copy in load_kv:
        copy.wait()
    fresh = project(normed_of(0), 0, 3)
    queries(0, fresh)
    for b in range(nb):
        k = fresh[:, b, :, inner : 2 * inner].reshape(span, inner).astype(BF16)
        v = fresh[:, b, :, 2 * inner :].reshape(span, inner).astype(BF16)
        kbuf[b, 2 * C * span :] = k
        vbuf[b, 2 * C * span :] = v
        fk_ref[b] = k
        fv_ref[b] = v
    for b in range(nb):

        def keep(at, o):
            own_o[b, :, at] = o

        own_s[b] = attend(qall[0, b], b, span, keep)
    load_ow.wait()
    for b in range(nb):
        for copy in back[b]:
            copy.wait_recv()
        helds = [own_s[b]] + [in_o[d, b, :, inner:].astype(F32) for d in range(1, NX)]
        for pair in range(inner // (2 * HD)):
            at = slice(pair * 2 * HD, (pair + 1) * 2 * HD)

            def spread_of(held, base):
                one_of = held[:, base + pair * 2 : base + pair * 2 + 1]
                two_of = held[:, base + pair * 2 + 1 : base + pair * 2 + 2]
                return jnp.where(half, one_of, two_of)

            parts = [own_o[b, :, at]] + [in_o[d, b, :, at].astype(F32) for d in range(1, NX)]
            peaks = [spread_of(held, 0) for held in helds]
            top = functools.reduce(jnp.maximum, peaks)
            num, den = 0.0, 0.0
            for held, o, peak in zip(helds, parts, peaks):
                factor = jnp.exp(peak - top)
                num = num + o * factor
                den = den + (spread_of(held, 32) + spread_of(held, 64)) * factor
            attn[b, :, at] = (num / den).astype(BF16)
        hb = hfull[0].reshape(rows, nb, cols, channels)[:, b].reshape(span, channels)
        mixed_ref[b] = (hb + jnp.dot(attn[b], ow[...], preferred_element_type=F32)).astype(BF16)

    beside_each(lambda copy: copy.wait_send(), lambda n: n)
    for k in range(1, C):
        for part in pieces:
            each(k, part, lambda copy: copy.wait_send(), 1)
    for copy in started:
        copy.wait_send()


def body(
    latent,
    timestep,
    gn_gain,
    gn_bias,
    conv_weight,
    conv_bias,
    time_weight,
    ln_gain,
    q_weight,
    k_weight,
    v_weight,
    out_weight,
    stale_keys,
    stale_values,
):
    batch, rows, cols, channels = latent.shape
    inner = q_weight.shape[1]
    R, C = lax.axis_size("row"), lax.axis_size("col")
    NX = R // PAIR
    span = rows * cols
    wide = conv_weight.shape[3]
    count_all = span * R * C * (channels // GROUPS)
    rest = wide % 128
    if wide // 128 == 1 and rest and 128 % rest == 0 and batch * span * rest % (16 * 128) == 0:
        block = (batch * span + batch * span * rest // 128, 128)
    else:
        block = (batch * span, wide)
    vm = pl.BlockSpec(memory_space=pltpu.VMEM)
    hbm = pl.BlockSpec(memory_space=pl.ANY)
    dma = pltpu.SemaphoreType.DMA
    mixed, fresh_k, fresh_v = pl.pallas_call(
        functools.partial(kernel, (R, C, NX, rows, cols, channels, inner, count_all)),
        out_shape=(
            pltpu.VMEM((batch, span, channels), BF16),
            pltpu.VMEM((batch, span, inner), BF16),
            pltpu.VMEM((batch, span, inner), BF16),
        ),
        in_specs=[hbm] * 14,
        out_specs=(vm, vm, vm),
        scratch_shapes=[
            pltpu.SMEM(timestep.shape, jnp.int32),
            pltpu.VMEM((channels,), F32),
            pltpu.VMEM((channels,), F32),
            pltpu.VMEM((channels,), F32),
            pltpu.VMEM((channels,), F32),
            pltpu.VMEM((R, batch, rows, cols, channels), BF16),
            pltpu.VMEM((2, batch, rows, channels), BF16),
            pltpu.VMEM((PAIR, NX, 2, batch, rows, channels), BF16),
            pltpu.VMEM(time_weight.shape, BF16),
            pltpu.VMEM((3, R * rows + 2, batch * cols, channels), BF16),
            pltpu.VMEM((3, 3, wide, channels), BF16),
            pltpu.VMEM((channels, 3 * inner), BF16),
            pltpu.VMEM((inner, channels), BF16),
            pltpu.VMEM((3, R, 8, 128), F32),
            pltpu.VMEM((C, 8, 128), F32),
            pltpu.VMEM((PAIR, NX) + block, BF16),
            pltpu.VMEM((R, NX) + block, BF16),
            pltpu.VMEM((NX, batch * span, channels), F32),
            pltpu.VMEM((batch, (2 * C + 1) * span, inner), BF16),
            pltpu.VMEM((batch, (2 * C + 1) * span, inner), BF16),
            pltpu.VMEM((NX, batch, span, inner), BF16),
            pltpu.VMEM((batch, span, inner), F32),
            pltpu.VMEM((batch, span, 128), F32),
            pltpu.VMEM((NX, batch, span, inner + 128), BF16),
            pltpu.VMEM((NX, batch, span, inner + 128), BF16),
            pltpu.VMEM((batch, span, inner), BF16),
            dma((14,)),
            dma((batch + 3, R)),
            dma((batch + 3, R)),
            dma((1, C)),
            dma((1, C)),
            dma((C, 2, 2, batch)),
            dma((C, 2, 2, batch)),
            dma((2, NX)),
            dma((2, NX)),
            dma((2, R)),
            dma((2, R)),
            dma((2, batch)),
            dma((2, batch)),
            dma((batch, NX)),
            dma((batch, NX)),
            dma((NX, NX, PAIR)),
            dma((NX, NX, PAIR)),
        ],
        compiler_params=pltpu.CompilerParams(
            collective_id=0, has_side_effects=True, vmem_limit_bytes=56 * 1024 * 1024
        ),
    )(
        timestep,
        gn_gain,
        gn_bias,
        ln_gain,
        conv_bias,
        latent,
        time_weight,
        conv_weight.transpose(0, 1, 3, 2),
        q_weight,
        k_weight,
        v_weight,
        out_weight,
        stale_keys.reshape(batch, span, inner),
        stale_values.reshape(batch, span, inner),
    )
    held = (pltpu.with_memory_space_constraint(x, pltpu.VMEM) for x in (mixed, fresh_k, fresh_v))
    mixed, fresh_k, fresh_v = pl.pallas_call(
        finish,
        out_shape=tuple(jax.ShapeDtypeStruct(x.shape, x.dtype) for x in (mixed, fresh_k, fresh_v)),
        in_specs=[vm] * 3,
        out_specs=(hbm,) * 3,
        scratch_shapes=[dma((3,))],
    )(*held)
    return (
        mixed.reshape(batch, rows, cols, channels),
        fresh_k.reshape(batch, rows, cols, inner),
        fresh_v.reshape(batch, rows, cols, inner),
    )


def solution(mesh):
    placed = (
        P("parts", "row", "col", None),
        P("parts"),
        P(),
        P(),
        P(None, None, None, "row"),
        P(),
        P(),
        P(),
        P(),
        P(),
        P(),
        P(),
        P("parts", "row", "col", None),
        P("parts", "row", "col", None),
    )
    return jax.shard_map(
        body,
        mesh=mesh,
        in_specs=placed,
        out_specs=(
            P("parts", "row", "col", None),
            P("parts", "row", "col", None),
            P("parts", "row", "col", None),
        ),
        check_vma=False,
    )
```
